256 devices in a mesh: dp: 16 (over z, core), tensor: 8 (over y, x_hi), mp: 2 (over x_lo).
Axes of the slice: x: 4 (x_hi: 2, x_lo: 2; x = x_hi * 2 + x_lo), y: 4, z: 8, core: 2. Of those that a mesh axis runs over, the one named last changes fastest.
Arguments:
- step_embeds: bfloat16 [2, 512, 32, 8192], P('mp', 'dp', None, 'tensor'), may hold values from -6 to 6
- step_len: int32 [512], replicated, may hold values from 8 to 32, as said below
- leaf_of_step: int32 [512], replicated, may hold values from 0 to 63, as said below
- cache_len: int32 [64], P('dp'), may hold values from 96 to 768, as said below
- caches: bfloat16 [2, 64, 768, 2048], P('mp', 'dp', None, 'tensor'), may hold values from -500 to 500
- norm_gain: float32 [2, 8192], P('mp'), may hold values from 0.1 to 1.9
- qkv_weight: bfloat16 [2, 8192, 6144], P('mp', 'dp', 'tensor'), may hold values from -0.1875 to 0.1875
- score_weight: float32 [2, 4096], P('mp', 'tensor'), may hold values from -0.09375 to 0.09375
Outputs:
- contexts: bfloat16 [2, 64, 8, 32, 4096], P('mp', 'dp', None, None, 'tensor')
- step_value: float32 [64, 8], P('dp')
The draws below stay inside these ranges and needn't reach their ends.
Inputs may be any that keep to these rules, and one draw needn't show every extreme that they name: `leaf_of_step`: every leaf is named by exactly 8 steps, and each aligned block of 32 steps names the leaves of every aligned block of 4 leaves equally often. `step_len`: some step has all 32 tokens. `cache_len`: some leaf fills all 768 cache positions.
All inputs are finite; a program needn't handle non-finite values.
Results may differ from the reference program's by a relative error of at most 0.0049.
The reference program's roundings to bfloat16 on the way count: a program that leaves them out, or rounds other values in their place, can miss the bound.
Values may be sent and summed in bfloat16 or wider, within the bound.
No kernel may reach another device: no remote copies, remote signals or barrier semaphores. Data moves between devices by JAX's collectives and lax.ppermute only.
A program may use at most 192 MiB of HBM per device.

```python
import jax
import jax.numpy as jnp
from jax import lax

D = 8192
KVH = 8
HD = 128
HQ = 32
SPL = 8
SMAX = 32
CTX = 768
LEAF_DEV = 4
QKV = 6144
STEP_DEV = 32
LEAVES = 64
STEPS = 512


def draw_leaf_of_step(key, part):
    part_count = STEPS // STEP_DEV
    per_peer = STEP_DEV // part_count
    send_keys = jax.random.split(jax.random.fold_in(key, 11), part_count)
    slot_of = jax.vmap(lambda sub_key: jax.random.permutation(sub_key, STEP_DEV))(send_keys)
    owner = slot_of // per_peer
    incoming = jnp.arange(part_count, dtype=jnp.int32)[:, None] * per_peer + slot_of % per_peer
    recv_keys = jax.random.split(jax.random.fold_in(key, 12), part_count)
    seating = jax.vmap(lambda sub_key: jax.random.permutation(sub_key, STEP_DEV))(recv_keys)
    seat_of = seating[owner, incoming]
    leaves = owner * LEAF_DEV + seat_of // SPL
    return leaves.reshape(STEPS).astype(jnp.int32)


def draw_step_len(key, part):
    drawn = jax.random.randint(jax.random.fold_in(key, 21), (STEPS,), SMAX // 4, SMAX + 1)
    chosen = jax.random.randint(jax.random.fold_in(key, 22), (), 0, STEPS)
    return jnp.where(jnp.arange(STEPS) == chosen, SMAX, drawn).astype(jnp.int32)


def draw_cache_len(key, part):
    drawn = jax.random.randint(jax.random.fold_in(key, 23), (LEAVES,), CTX // 8, CTX + 1)
    chosen = jax.random.randint(jax.random.fold_in(key, 24), (), 0, LEAVES)
    return jnp.where(jnp.arange(LEAVES) == chosen, CTX, drawn).astype(jnp.int32)


def draw_caches(key, part):
    array_shape = (2, LEAVES, CTX, 2 * KVH * HD)
    drawn = jax.random.normal(jax.random.fold_in(key, 35), array_shape, jnp.float32)
    return jnp.clip(drawn, -6.0, 6.0).astype(jnp.bfloat16)


def level_of(rng, shape, cuts, smallest, high):
    factor_of = 1.0
    for dim, shards_of in cuts:
        heights = jax.random.uniform(jax.random.fold_in(jax.random.fold_in(rng, 6), dim), (shards_of,), jnp.float32, smallest / len(cuts), high / len(cuts))
        factor_of = factor_of * jnp.repeat(jnp.exp(heights), shape[dim] // shards_of).reshape((-1,) + (1,) * (len(shape) - 1 - dim))
    return factor_of


def gaussian(rng, extent, scale, reach, cuts=(), kind=jnp.bfloat16):
    loudness = level_of(rng, extent, cuts, -0.22, 0.18) if cuts else 1.0
    result = jax.random.normal(rng, extent, jnp.float32) * scale * loudness
    return jnp.minimum(jnp.maximum(result, -reach), reach).astype(kind)


def setup_inputs(seed: int = 0) -> dict:
    keys = jax.random.split(jax.random.key(seed), 9)
    return {
        "step_embeds": gaussian(keys[0], (2, STEPS, SMAX, D), 1.0, 6.0, ((0, 2), (1, 16), (3, 8))),
        "step_len": draw_step_len(jax.random.fold_in(keys[8], 71), 0),
        "leaf_of_step": draw_leaf_of_step(jax.random.fold_in(keys[8], 71), 0),
        "cache_len": draw_cache_len(jax.random.fold_in(keys[8], 71), 0),
        "caches": draw_caches(jax.random.fold_in(keys[8], 71), 0),
        "norm_gain": jnp.clip(1.0 + 0.18 * jax.random.normal(keys[5], (2, D), jnp.float32), 0.1, 1.9),
        "qkv_weight": gaussian(keys[6], (2, D, QKV), (D // 8) ** -0.5, 0.1875, ((0, 2), (1, 16), (2, 8))),
        "score_weight": gaussian(keys[7], (2, HQ * HD), (HQ * HD) ** -0.5, 0.09375, ((0, 2), (1, 8)), jnp.float32),
    }


prior_weight = 0.5
norm_eps = 1e-05

def one_model(embeds, lengths, cache_lens, cache, gain, weight, score_vec, order):
    group_size = HQ // KVH

    def per_leaf(inputs):
        leaf_steps, leaf_cache, leaf_len = inputs
        rows = embeds[leaf_steps]
        step_lens = lengths[leaf_steps]
        as_float = rows.astype(jnp.float32)
        inverse_rms = lax.rsqrt(lax.optimization_barrier(jnp.mean(as_float * as_float, axis=-1, keepdims=True)) + norm_eps)
        normed = (as_float * inverse_rms * gain).astype(jnp.bfloat16)
        projected = jnp.dot(normed.reshape(SPL * SMAX, D), weight, preferred_element_type=jnp.float32).astype(jnp.bfloat16)
        projected = projected.reshape(SPL, SMAX, KVH, group_size + 2, HD)
        queries = projected[:, :, :, :group_size].astype(jnp.float32)
        key_own = projected[:, :, :, group_size].astype(jnp.float32)
        value_own = projected[:, :, :, group_size + 1].astype(jnp.float32)
        cache_rows = leaf_cache.reshape(CTX, KVH, 2, HD)
        key_cache = cache_rows[:, :, 0].astype(jnp.float32)
        value_cache = cache_rows[:, :, 1].astype(jnp.float32)
        scale_q = HD ** (-0.5)
        own_scores = jnp.einsum('sikgh,sjkh->sikgj', queries, key_own) * scale_q
        positions = jnp.arange(SMAX, dtype=jnp.int32)
        causal = positions[None, :] <= positions[:, None]
        own_scores = jnp.where(causal[:, None, None, :], own_scores, -jnp.inf)
        far_scores = jnp.einsum('sikgh,ckh->sikgc', queries, key_cache) * scale_q
        is_live = jnp.arange(CTX, dtype=jnp.int32) < leaf_len
        far_scores = jnp.where(is_live, far_scores, -jnp.inf)
        row_max = jnp.maximum(own_scores.max(-1), far_scores.max(-1))
        own_probs = jnp.exp(own_scores - row_max[..., None])
        far_probs = jnp.exp(far_scores - row_max[..., None])
        total = own_probs.sum(-1) + far_probs.sum(-1)
        own_b = own_probs.astype(jnp.bfloat16).astype(jnp.float32)
        far_b = far_probs.astype(jnp.bfloat16).astype(jnp.float32)
        context = jnp.einsum('sikgj,sjkh->sikgh', own_b, value_own) + jnp.einsum('sikgc,ckh->sikgh', far_b, value_cache)
        context = context / total[..., None]
        is_valid = positions[None, :] < step_lens[:, None]
        context = jnp.where(is_valid[:, :, None, None, None], context, 0.0)
        flat = context.reshape(SPL, SMAX, HQ * HD)
        last_token = (positions[None, :] == step_lens[:, None] - 1).astype(jnp.float32)
        last_context = lax.optimization_barrier(jnp.sum(last_token[:, :, None] * flat, axis=1))
        score = lax.optimization_barrier(jnp.sum(last_context * score_vec, axis=-1))
        return (flat.astype(jnp.bfloat16), score)
    return lax.map(per_leaf, (order, cache, cache_lens))

def reference(step_embeds, step_len, leaf_of_step, cache_len, caches, norm_gain, qkv_weight, score_weight):
    step_index = jnp.arange(STEPS, dtype=jnp.int32)
    order = jnp.argsort(leaf_of_step * STEPS + step_index).astype(jnp.int32).reshape(LEAVES, SPL)
    policy_ctx, policy_score = one_model(step_embeds[0], step_len, cache_len, caches[0], norm_gain[0], qkv_weight[0], score_weight[0], order)
    reward_ctx, reward_score = one_model(step_embeds[1], step_len, cache_len, caches[1], norm_gain[1], qkv_weight[1], score_weight[1], order)
    contexts = jnp.stack([policy_ctx, reward_ctx], axis=0)
    step_value = prior_weight * policy_score + reward_score
    return (contexts, step_value)
```

```python
import functools

import jax
import jax.numpy as jnp
from jax import lax
from jax.experimental import pallas as pl
from jax.experimental.pallas import tpu as pltpu
from jax.sharding import PartitionSpec as P


KVH = 8
HD = 128
HQ = 32
GROUP = HQ // KVH

prior_weight = 0.5
norm_eps = 1e-05
LOG2E = 1.4426950408889634


def sent_to_all(value, axis):
    length = lax.axis_size(axis)
    return lax.all_to_all(
        jnp.broadcast_to(value[None], (length, *value.shape)), axis, 0, 0, tiled=True
    )


def y_shift(value, hop):
    pairs = [(y * 2 + h, ((y + hop) % 4) * 2 + h) for y in range(4) for h in range(2)]
    return lax.ppermute(value, "tensor", pairs)


def x_swap(value):
    return lax.ppermute(value, "tensor", [(t, t ^ 1) for t in range(8)])


def z_shift(value, hop):
    pairs = [(z * 2 + c, ((z + hop) % 8) * 2 + c) for z in range(8) for c in range(2)]
    return lax.ppermute(value, "dp", pairs)


def core_swap(value):
    return lax.ppermute(value, "dp", [(d, d ^ 1) for d in range(16)])


def ring_weights(shard):
    half = shard.shape[0] // 2
    up, down = shard, shard
    found = [((0, 0), 0, shard)]
    for step in range(1, 4):
        up, down = z_shift(up, 1), z_shift(down, -1)
        found += [((8 - step, step), 0, up), ((step, step), 0, down)]
    found += [
        ((4, 4), 0, z_shift(up[:half], 1)),
        ((4, 4), half, z_shift(down[half:], -1)),
    ]
    shards = []
    for (hop, step), first, value in found:
        shards.append(((hop, 0, first), value))
        shards.append(((hop, 1, first), core_swap(value)))
    return shards


def mm_kernel(tp_ref, place_ref, sums_ref, gain_ref, *rest, halves, shards, has_acc, last, width):
    count = len(halves)
    copies = sum(2 if h else 1 for h in halves)
    weights, rest = rest[: len(shards)], rest[len(shards) :]
    pieces, rest = rest[:copies], rest[copies:]
    if has_acc:
        acc_in, rest = rest[0], rest[1:]
    out_ref, xbuf, wbuf, acc, xsem, wsem, asem = rest
    rows = xbuf.shape[1]
    half = rows // 2
    position = 0
    for p, is_half in enumerate(halves):
        if is_half:
            for k in range(2):
                pltpu.make_async_copy(
                    pieces[position + k], xbuf.at[p, pl.ds(k * half, half)], xsem.at[p]
                ).start()
            position += 2
        else:
            pltpu.make_async_copy(pieces[position], xbuf.at[p], xsem.at[p]).start()
            position += 1
    for ref, (hop, other, first) in zip(weights, shards):
        block = place_ref[hop]
        start = place_ref[8 + other] + first

        def fetch(ref=ref, block=block, start=start):
            pltpu.make_async_copy(
                ref,
                wbuf.at[block, pl.ds(pl.multiple_of(start, 256), ref.shape[0])],
                wsem.at[block],
            ).start()

        if count == 8:
            fetch()
        else:
            wanted = tp_ref[0] == block
            for p in range(1, count):
                wanted = wanted | (tp_ref[p] == block)
            pl.when(wanted)(fetch)
    if has_acc:
        load = pltpu.make_async_copy(acc_in, acc, asem)
        load.start()
    total = jnp.sum(jnp.transpose(sums_ref[...]), axis=1, keepdims=True)
    inverse = lax.rsqrt(total * (1.0 / width) + norm_eps)
    if has_acc:
        load.wait()
    else:
        acc[...] = jnp.zeros_like(acc)

    def visit(p, carry):
        block = tp_ref[p]
        pltpu.make_async_copy(xbuf.at[p], xbuf.at[p], xsem.at[p]).wait()
        pltpu.make_async_copy(wbuf.at[block], wbuf.at[block], wsem.at[block]).wait()
        gain = gain_ref[pl.ds(block, 1), :]
        normed = (xbuf[p].astype(jnp.float32) * inverse * gain).astype(jnp.bfloat16)
        acc[...] += jnp.dot(normed, wbuf[block], preferred_element_type=jnp.float32)
        return carry

    lax.fori_loop(0, count, visit, 0)
    if last:
        out_ref[...] = acc[...].astype(out_ref.dtype)
    else:
        out_ref[...] = acc[...]


def project(tp, place, sums, gain, weights, pieces, acc=None, last=True):
    shards = tuple(key for key, _ in weights)
    weights = [value for _, value in weights]
    blocks, feats = gain.shape
    columns = weights[0].shape[1]
    rows = sums.shape[1]
    halves = tuple(isinstance(piece, tuple) for piece in pieces)
    flat = []
    for piece in pieces:
        flat.extend(piece if isinstance(piece, tuple) else (piece,))
    count = len(pieces)
    smem = pl.BlockSpec(memory_space=pltpu.SMEM)
    vmem = pl.BlockSpec(memory_space=pltpu.VMEM)
    anyspace = pl.BlockSpec(memory_space=pl.ANY)
    extra = [] if acc is None else [acc]
    return pl.pallas_call(
        functools.partial(
            mm_kernel,
            halves=halves,
            shards=shards,
            has_acc=acc is not None,
            last=last,
            width=feats * blocks,
        ),
        out_shape=jax.ShapeDtypeStruct((rows, columns), jnp.bfloat16 if last else jnp.float32),
        in_specs=[smem, smem, vmem, vmem]
        + [anyspace] * (len(weights) + len(flat) + len(extra)),
        out_specs=vmem,
        scratch_shapes=[
            pltpu.VMEM((count, rows, feats), jnp.bfloat16),
            pltpu.VMEM((blocks, feats, columns), jnp.bfloat16),
            pltpu.VMEM((rows, columns), jnp.float32),
            pltpu.SemaphoreType.DMA((count,)),
            pltpu.SemaphoreType.DMA((blocks,)),
            pltpu.SemaphoreType.DMA,
        ],
        compiler_params=pltpu.CompilerParams(vmem_limit_bytes=44 << 20),
        cost_estimate=pl.CostEstimate(
            flops=2 * rows * columns * feats * count,
            bytes_accessed=2 * count * feats * (rows + columns),
            transcendentals=0,
        ),
        name="project",
    )(tp, place, sums, gain, *weights, *flat, *extra)


def attend_kernel(meta_ref, clen_ref, rows_hbm, cache_ref, score_ref, *rest, seq, has_in):
    if has_in:
        rest = rest[1:]
    ctx_ref, value_ref, rows_ref, obuf, rsems, sems = rest
    steps = rows_ref.shape[0]
    positions = cache_ref.shape[1]
    wide = GROUP * seq
    factor = (HD ** (-0.5)) * LOG2E
    token = lax.broadcasted_iota(jnp.int32, (wide, 1), 0) % seq
    column = lax.broadcasted_iota(jnp.int32, (1, positions), 1)
    causal = lax.broadcasted_iota(jnp.int32, (wide, seq), 1) <= (
        lax.broadcasted_iota(jnp.int32, (wide, seq), 0) % seq
    )
    value_ref[...] = jnp.zeros_like(value_ref)
    weights = jnp.concatenate(
        [jnp.broadcast_to(score_ref[g : g + 1, :], (seq, HD)) for g in range(GROUP)], axis=0
    )
    contract = (((1,), (1,)), ((), ()))

    together = 4

    def load(group):
        part = pl.ds(group * together, together)
        return pltpu.make_async_copy(rows_hbm.at[part], rows_ref.at[part], rsems.at[group])

    for group in range(steps // together):
        load(group).start()

    def visit(group, carry):
        load(group).wait()
        at = [group * together + k for k in range(together)]
        leaf = [meta_ref[0, i] for i in at]
        slot = [meta_ref[1, i] for i in at]
        length = [meta_ref[2, i] for i in at]
        far, own = [], []
        for i, one in zip(at, leaf):
            queries = jnp.concatenate(
                [rows_ref[i, :, g * HD : (g + 1) * HD] for g in range(GROUP)], axis=0
            )
            key_own = rows_ref[i, :, GROUP * HD : (GROUP + 1) * HD]
            far.append(
                lax.dot_general(
                    queries, cache_ref[one, :, :HD], contract, preferred_element_type=jnp.float32
                )
            )
            own.append(
                lax.dot_general(queries, key_own, contract, preferred_element_type=jnp.float32)
            )
        far = [
            f + jnp.where(column < clen_ref[one], 0.0, -jnp.inf) for f, one in zip(far, leaf)
        ]
        own = [jnp.where(causal, o, -jnp.inf) for o in own]
        top = [
            jnp.maximum(jnp.max(f, axis=1, keepdims=True), jnp.max(o, axis=1, keepdims=True))
            for f, o in zip(far, own)
        ]
        far = [jnp.exp2((f - t) * factor) for f, t in zip(far, top)]
        own = [jnp.exp2((o - t) * factor) for o, t in zip(own, top)]
        total = [
            jnp.sum(f, axis=1, keepdims=True) + jnp.sum(o, axis=1, keepdims=True)
            for f, o in zip(far, own)
        ]
        context = [
            jnp.dot(
                f.astype(jnp.bfloat16), cache_ref[one, :, HD:], preferred_element_type=jnp.float32
            )
            + jnp.dot(
                o.astype(jnp.bfloat16),
                rows_ref[i, :, (GROUP + 1) * HD :],
                preferred_element_type=jnp.float32,
            )
            for f, o, one, i in zip(far, own, leaf, at)
        ]
        for c, t, i, place, count in zip(context, total, at, slot, length):
            c = jnp.where(token < count, c * (1.0 / t), 0.0)
            for g in range(GROUP):
                obuf[i, :, g * HD : (g + 1) * HD] = c[g * seq : (g + 1) * seq].astype(
                    jnp.bfloat16
                )
            pltpu.make_async_copy(obuf.at[i], ctx_ref.at[place], sems.at[i]).start()
            scored = jnp.where(token == count - 1, c * weights, 0.0)
            scored = jnp.sum(jnp.sum(scored, axis=0, keepdims=True), axis=1, keepdims=True)
            value_ref[pl.ds(place, 1), :] = jnp.broadcast_to(scored, (1, value_ref.shape[1]))
        return carry

    lax.fori_loop(0, steps // together, visit, 0)
    for i in range(steps):
        pltpu.make_async_copy(obuf.at[i], ctx_ref.at[meta_ref[1, i]], sems.at[i]).wait()


def attend(meta, cache_len, rows, cache, score, slots, earlier=None):
    steps, seq, _ = rows.shape
    smem = pl.BlockSpec(memory_space=pltpu.SMEM)
    vmem = pl.BlockSpec(memory_space=pltpu.VMEM)
    anyspace = pl.BlockSpec(memory_space=pl.ANY)
    extra = [] if earlier is None else [earlier]
    return pl.pallas_call(
        functools.partial(attend_kernel, seq=seq, has_in=earlier is not None),
        out_shape=(
            jax.ShapeDtypeStruct((slots, seq, GROUP * HD), jnp.bfloat16),
            jax.ShapeDtypeStruct((slots, HD), jnp.float32),
        ),
        in_specs=[smem, smem, anyspace, vmem, vmem] + [anyspace] * len(extra),
        out_specs=(anyspace, vmem),
        scratch_shapes=[
            pltpu.VMEM(rows.shape, jnp.bfloat16),
            pltpu.VMEM((steps, seq, GROUP * HD), jnp.bfloat16),
            pltpu.SemaphoreType.DMA((steps // 4,)),
            pltpu.SemaphoreType.DMA((steps,)),
        ],
        input_output_aliases={} if earlier is None else {5: 0},
        compiler_params=pltpu.CompilerParams(vmem_limit_bytes=24 << 20),
        cost_estimate=pl.CostEstimate(
            flops=4 * steps * GROUP * seq * cache.shape[1] * HD,
            bytes_accessed=2 * (rows.size + cache.size + slots * seq * GROUP * HD),
            transcendentals=steps * GROUP * seq * cache.shape[1],
        ),
        name="attend",
    )(meta, cache_len, rows, cache, score, *extra)


def staged(
    step_embeds, step_len, leaf_of_step, cache_len, caches, norm_gain, qkv_weight, score_weight
):
    embeds = step_embeds[0]
    steps_here, seq, feats = embeds.shape
    leaves_here = cache_len.shape[0]
    per_leaf = steps_here // leaves_here
    peers = lax.axis_size("dp")
    me = lax.axis_index("dp")
    tensor = lax.axis_index("tensor")
    rows = peers * seq

    weights = ring_weights(qkv_weight[0])
    z, core = me // 2, me % 2
    place = jnp.concatenate(
        [
            (z + jnp.arange(8, dtype=jnp.int32)) % 8,
            jnp.stack([core, 1 - core]) * qkv_weight.shape[1],
        ]
    ).astype(jnp.int32)

    leaves = leaf_of_step.reshape(peers, steps_here)
    lengths = step_len.reshape(peers, steps_here)
    index = jnp.arange(steps_here, dtype=jnp.int32)
    earlier = index[None, :] < index[:, None]
    mine = lax.dynamic_index_in_dim(leaves, me, 0, keepdims=False) // leaves_here
    same = mine[None, :] == mine[:, None]
    turn = jnp.sum(same & earlier, axis=1)
    to_peer = mine[None, :] == jnp.arange(peers, dtype=jnp.int32)[:, None]
    send = [
        jnp.sum(jnp.where(to_peer & (turn == s)[None, :], index[None, :], 0), axis=1)
        for s in range(2)
    ]
    early_rows = embeds[send[0]].reshape(rows, feats)
    late_rows = embeds[send[1]]
    late_rows = lax.all_to_all(late_rows, "dp", 0, 0, tiled=True).reshape(rows, feats)

    here = (leaves // leaves_here) == me
    ordinal = jnp.sum(here[:, None, :] & earlier[None], axis=2)
    marks = jnp.stack([here & (ordinal == s) for s in range(2)])
    ids = index[None, :] + steps_here * jnp.arange(peers, dtype=jnp.int32)[:, None]
    arrive_id = jnp.sum(jnp.where(marks, ids[None], 0), axis=2).reshape(-1)
    arrive_leaf = jnp.sum(jnp.where(marks, leaves[None], 0), axis=2).reshape(-1)
    arrive_leaf = arrive_leaf - me * leaves_here
    arrive_len = jnp.sum(jnp.where(marks, lengths[None], 0), axis=2).reshape(-1)
    rank = jnp.sum(
        (arrive_leaf[None, :] == arrive_leaf[:, None])
        & (arrive_id[None, :] < arrive_id[:, None]),
        axis=1,
    )
    slot = jnp.clip(arrive_leaf * per_leaf + rank, 0, steps_here - 1)
    arrive_leaf = jnp.clip(arrive_leaf, 0, leaves_here - 1)
    meta = jnp.stack([arrive_leaf, slot, arrive_len]).astype(jnp.int32)

    a, b = early_rows, late_rows
    a_x = x_swap(a)
    a_left, a_right = y_shift(a, 1), y_shift(a, -1)
    b_left, b_right = y_shift(b, 1), y_shift(b, -1)
    b_x = x_swap(b)
    ax_left = y_shift(a_x, 1)
    ax_right = y_shift(a_x, -1)
    a_far = y_shift(a_left, 1)
    ax_far = y_shift(ax_right, -1)
    bx_left = x_swap(b_left)
    bx_right = x_swap(b_right)
    b_far = y_shift(b_right, -1)
    bx_far = y_shift(bx_left, 1)

    squares = [
        jnp.sum(jnp.square(part.astype(jnp.float32)), axis=1) for part in (a, b)
    ]
    sums = sent_to_all(jnp.concatenate(squares), "tensor")
    sums_a, sums_b = sums[:, :rows], sums[:, rows:]

    y, h = tensor // 2, tensor % 2

    def owner(dy, dx):
        return ((y + dy) % 4) * 2 + ((h + dx) % 2)

    first = [owner(0, 0), owner(-1, 0), owner(1, 0), owner(0, 1), owner(-1, 1)]
    then = [owner(1, 1), owner(2, 0), owner(2, 1)]
    gain = norm_gain[0].reshape(-1, feats)
    out_a = project(
      jnp.stack(first + then).astype(jnp.int32),
      place,
      sums_a,
      gain,
      weights,
      [a, a_left, a_right, a_x, ax_left, ax_right, a_far, ax_far],
    )
    part_b = project(
      jnp.stack(first).astype(jnp.int32),
      place,
      sums_b,
      gain,
      weights,
      [b, b_left, b_right, b_x, bx_left],
      last=False,
    )
    out_b = project(
        jnp.stack(then).astype(jnp.int32), place, sums_b, gain, weights, [bx_right, b_far, bx_far], acc=part_b
    )

    out_a = lax.all_to_all(out_a.reshape(peers, seq, -1), "dp", 0, 0, tiled=True)
    out_b = out_b.reshape(peers, seq, -1)
    cache = caches[0]
    score = score_weight[0].reshape(GROUP, HD)
    context, value_b = attend(meta[:, peers:], cache_len, out_b, cache, score, steps_here)
    context, value_a = attend(
        meta[:, :peers], cache_len, out_a, cache, score, steps_here, earlier=context
    )
    contexts = context.reshape(1, leaves_here, per_leaf, seq, GROUP * HD)
    model_weight = jnp.where(lax.axis_index("mp") == 0, prior_weight, 1.0).astype(jnp.float32)
    partial = (value_a + value_b)[:, 0].reshape(leaves_here, per_leaf) * model_weight
    step_value = jnp.sum(sent_to_all(partial, ("tensor", "mp")), axis=0)
    return (contexts, step_value)


def solution(mesh):
    placed = (
        P("mp", "dp", None, "tensor"),
        P(),
        P(),
        P("dp"),
        P("mp", "dp", None, "tensor"),
        P("mp", None),
        P("mp", "dp", "tensor"),
        P("mp", "tensor"),
    )
    return jax.shard_map(
        staged,
        mesh=mesh,
        in_specs=placed,
        out_specs=(P("mp", "dp", None, None, "tensor"), P("dp", None)),
        check_vma=False,
    )
```

```python
import functools

import jax
import jax.numpy as jnp
from jax import lax
from jax.experimental import pallas as pl
from jax.experimental.pallas import tpu as pltpu
from jax.sharding import PartitionSpec as P


KVH = 8
HD = 128
HQ = 32
GROUP = HQ // KVH

prior_weight = 0.5
norm_eps = 1e-05
LOG2E = 1.4426950408889634


RING = (0, 7, 1, 6, 2, 5, 3, 4)
PLACES = ((0, 0), (-1, 0), (1, 0), (0, 1), (-1, 1), (1, 1), (2, 0), (2, 1))


def sent_to_all(value, axis):
    length = lax.axis_size(axis)
    return lax.all_to_all(
        jnp.broadcast_to(value[None], (length, *value.shape)), axis, 0, 0, tiled=True
    )


def y_shift(value, hop):
    pairs = [(y * 2 + h, ((y + hop) % 4) * 2 + h) for y in range(4) for h in range(2)]
    return lax.ppermute(value, "tensor", pairs)


def x_swap(value):
    return lax.ppermute(value, "tensor", [(t, t ^ 1) for t in range(8)])


def z_shift(value, hop):
    pairs = [(z * 2 + c, ((z + hop) % 8) * 2 + c) for z in range(8) for c in range(2)]
    return lax.ppermute(value, "dp", pairs)


def core_swap(value):
    return lax.ppermute(value, "dp", [(d, d ^ 1) for d in range(16)])


def ring_weights(shard):
    half = shard.shape[0] // 2
    up, down = shard, shard
    found = [((0, 0), 0, shard)]
    for step in range(1, 4):
        up, down = z_shift(up, 1), z_shift(down, -1)
        found += [((2 * step - 1, step), 0, up), ((2 * step, step), 0, down)]
    found += [
        ((7, 4), 0, z_shift(up[:half], 1)),
        ((7, 4), half, z_shift(down[half:], -1)),
    ]
    shards = []
    for (place, step), first, value in found:
        shards.append(((place, 0, first), value))
        shards.append(((place, 1, first), core_swap(value)))
    return shards


def mm_kernel(table_ref, sums_ref, gain_ref, *rest, row, count, shards, has_acc, last, width):
    weights, rest = rest[: len(shards)], rest[len(shards) :]
    pieces, rest = rest[:count], rest[count:]
    if has_acc:
        acc_in, rest = rest[0], rest[1:]
    out_ref, xbuf, wbuf, acc, inverse, high, low, xsem, wsem, asem = rest
    part = xbuf.shape[1] // 2
    for p in range(count):

        @pl.when(table_ref[row, 18 + p] > 0)
        def _(p=p):
            pltpu.make_async_copy(pieces[p], xbuf.at[p], xsem.at[p]).start()

    for k in range(8):
        mine = [(ref, key) for ref, key in zip(weights, shards) if key[0] == k]
        if mine:

            @pl.when(table_ref[row, k] >= 0)
            def _(k=k, mine=mine):
                for ref, (_, other, first) in mine:
                    start = pl.multiple_of(table_ref[row, 16 + other] + first, 256)
                    pltpu.make_async_copy(
                        ref, wbuf.at[k, pl.ds(start, ref.shape[0])], wsem.at[k]
                    ).start()

    if has_acc:
        load = pltpu.make_async_copy(acc_in, acc, asem)
        load.start()
    total = jnp.sum(jnp.transpose(sums_ref[...]), axis=1, keepdims=True)
    inverse[...] = lax.rsqrt(total * (1.0 / width) + norm_eps)
    if has_acc:
        load.wait()
    else:
        acc[...] = jnp.zeros_like(acc)
    used = table_ref[row, 34]
    upper, lower = pl.ds(0, part), pl.ds(part, part)

    def ready(i):
        p = table_ref[row, table_ref[row, 26 + i]]
        pltpu.make_async_copy(xbuf.at[p], xbuf.at[p], xsem.at[p]).wait()

    def normed(i, at):
        k = table_ref[row, 26 + i]
        gain = gain_ref[pl.ds(table_ref[row, 8 + k], 1), :]
        x = xbuf[table_ref[row, k], at, :].astype(jnp.float32)
        return (x * inverse[at, :] * gain).astype(jnp.bfloat16)

    def visit(i, carry):
        k = table_ref[row, 26 + i]
        following = jnp.minimum(i + 1, used - 1)
        pl.when(i + 1 < used)(lambda: ready(following))
        pltpu.make_async_copy(wbuf.at[k], wbuf.at[k], wsem.at[k]).wait()
        low[...] = normed(i, lower)
        acc[upper, :] += jnp.dot(high[...], wbuf[k], preferred_element_type=jnp.float32)
        high[...] = normed(following, upper)
        acc[lower, :] += jnp.dot(low[...], wbuf[k], preferred_element_type=jnp.float32)
        return carry

    @pl.when(used > 0)
    def _():
        ready(0)
        high[...] = normed(0, upper)
        lax.fori_loop(0, used, visit, 0)

    if last:
        out_ref[...] = acc[...].astype(out_ref.dtype)
    else:
        out_ref[...] = acc[...]


def project(table, row, sums, gain, weights, pieces, hops=8, acc=None, last=True):
    weights = [pair for pair in weights if pair[0][0] < hops]
    shards = tuple(key for key, _ in weights)
    weights = [value for _, value in weights]
    blocks, feats = gain.shape
    columns = weights[0].shape[1]
    rows = sums.shape[1]
    count = len(pieces)
    smem = pl.BlockSpec(memory_space=pltpu.SMEM)
    vmem = pl.BlockSpec(memory_space=pltpu.VMEM)
    anyspace = pl.BlockSpec(memory_space=pl.ANY)
    extra = [] if acc is None else [acc]
    typical = min(count, 4)
    return pl.pallas_call(
        functools.partial(
            mm_kernel,
            row=row,
            count=count,
            shards=shards,
            has_acc=acc is not None,
            last=last,
            width=feats * blocks,
        ),
        out_shape=jax.ShapeDtypeStruct((rows, columns), jnp.bfloat16 if last else jnp.float32),
        in_specs=[smem, vmem, vmem] + [anyspace] * (len(weights) + count + len(extra)),
        out_specs=vmem,
        scratch_shapes=[
            pltpu.VMEM((count, rows, feats), jnp.bfloat16),
            pltpu.VMEM((blocks, feats, columns), jnp.bfloat16),
            pltpu.VMEM((rows, columns), jnp.float32),
            pltpu.VMEM((rows, 1), jnp.float32),
            pltpu.VMEM((rows // 2, feats), jnp.bfloat16),
            pltpu.VMEM((rows // 2, feats), jnp.bfloat16),
            pltpu.SemaphoreType.DMA((count,)),
            pltpu.SemaphoreType.DMA((blocks,)),
            pltpu.SemaphoreType.DMA,
        ],
        compiler_params=pltpu.CompilerParams(vmem_limit_bytes=44 << 20),
        cost_estimate=pl.CostEstimate(
            flops=2 * rows * columns * feats * typical,
            bytes_accessed=2 * typical * feats * (rows + columns),
            transcendentals=0,
        ),
        name="project",
    )(table, sums, gain, *weights, *pieces, *extra)


def attend_kernel(meta_ref, clen_ref, rows_hbm, cache_hbm, score_ref, *rest, seq, has_in):
    if has_in:
        rest = rest[1:]
    ctx_ref, value_ref, rows_ref, cache_ref, obuf, rsems, csem, sems = rest
    steps = rows_ref.shape[0]
    fill = pltpu.make_async_copy(cache_hbm, cache_ref, csem)
    fill.start()
    positions = cache_ref.shape[1]
    wide = GROUP * seq
    factor = (HD ** (-0.5)) * LOG2E
    token = lax.broadcasted_iota(jnp.int32, (wide, 1), 0) % seq
    column = lax.broadcasted_iota(jnp.int32, (1, positions), 1)
    causal = lax.broadcasted_iota(jnp.int32, (wide, seq), 1) <= (
        lax.broadcasted_iota(jnp.int32, (wide, seq), 0) % seq
    )
    value_ref[...] = jnp.zeros_like(value_ref)
    weights = jnp.concatenate(
        [jnp.broadcast_to(score_ref[g : g + 1, :], (seq, HD)) for g in range(GROUP)], axis=0
    )
    contract = (((1,), (1,)), ((), ()))

    together = 4

    def load(group):
        part = pl.ds(group * together, together)
        return pltpu.make_async_copy(rows_hbm.at[part], rows_ref.at[part], rsems.at[group])

    for group in range(steps // together):
        load(group).start()

    def visit(group, carry):
        load(group).wait()
        at = [group * together + k for k in range(together)]
        leaf = [meta_ref[0, i] for i in at]
        slot = [meta_ref[1, i] for i in at]
        length = [meta_ref[2, i] for i in at]
        far, own = [], []
        for i, one in zip(at, leaf):
            queries = jnp.concatenate(
                [rows_ref[i, :, g * HD : (g + 1) * HD] for g in range(GROUP)], axis=0
            )
            key_own = rows_ref[i, :, GROUP * HD : (GROUP + 1) * HD]
            far.append(
                lax.dot_general(
                    queries, cache_ref[one, :, :HD], contract, preferred_element_type=jnp.float32
                )
            )
            own.append(
                lax.dot_general(queries, key_own, contract, preferred_element_type=jnp.float32)
            )
        far = [
            f + jnp.where(column < clen_ref[one], 0.0, -jnp.inf) for f, one in zip(far, leaf)
        ]
        own = [jnp.where(causal, o, -jnp.inf) for o in own]
        top = [
            jnp.maximum(jnp.max(f, axis=1, keepdims=True), jnp.max(o, axis=1, keepdims=True))
            for f, o in zip(far, own)
        ]
        far = [jnp.exp2((f - t) * factor) for f, t in zip(far, top)]
        own = [jnp.exp2((o - t) * factor) for o, t in zip(own, top)]
        total = [
            jnp.sum(f, axis=1, keepdims=True) + jnp.sum(o, axis=1, keepdims=True)
            for f, o in zip(far, own)
        ]
        context = [
            jnp.dot(
                f.astype(jnp.bfloat16), cache_ref[one, :, HD:], preferred_element_type=jnp.float32
            )
            + jnp.dot(
                o.astype(jnp.bfloat16),
                rows_ref[i, :, (GROUP + 1) * HD :],
                preferred_element_type=jnp.float32,
            )
            for f, o, one, i in zip(far, own, leaf, at)
        ]
        for c, t, i, place, count in zip(context, total, at, slot, length):
            c = jnp.where(token < count, c * (1.0 / t), 0.0)
            for g in range(GROUP):
                obuf[i, :, g * HD : (g + 1) * HD] = c[g * seq : (g + 1) * seq].astype(
                    jnp.bfloat16
                )
            pltpu.make_async_copy(obuf.at[i], ctx_ref.at[place], sems.at[i]).start()
            scored = jnp.where(token == count - 1, c * weights, 0.0)
            scored = jnp.sum(jnp.sum(scored, axis=0, keepdims=True), axis=1, keepdims=True)
            value_ref[pl.ds(place, 1), :] = jnp.broadcast_to(scored, (1, value_ref.shape[1]))
        return carry

    fill.wait()
    lax.fori_loop(0, steps // together, visit, 0)
    for i in range(steps):
        pltpu.make_async_copy(obuf.at[i], ctx_ref.at[meta_ref[1, i]], sems.at[i]).wait()


def attend(meta, cache_len, rows, cache, score, slots, earlier=None):
    steps, seq, _ = rows.shape
    smem = pl.BlockSpec(memory_space=pltpu.SMEM)
    vmem = pl.BlockSpec(memory_space=pltpu.VMEM)
    anyspace = pl.BlockSpec(memory_space=pl.ANY)
    extra = [] if earlier is None else [earlier]
    return pl.pallas_call(
        functools.partial(attend_kernel, seq=seq, has_in=earlier is not None),
        out_shape=(
            jax.ShapeDtypeStruct((slots, seq, GROUP * HD), jnp.bfloat16),
            jax.ShapeDtypeStruct((slots, HD), jnp.float32),
        ),
        in_specs=[smem, smem, anyspace, anyspace, vmem] + [anyspace] * len(extra),
        out_specs=(anyspace, vmem),
        scratch_shapes=[
            pltpu.VMEM(rows.shape, jnp.bfloat16),
            pltpu.VMEM(cache.shape, jnp.bfloat16),
            pltpu.VMEM((steps, seq, GROUP * HD), jnp.bfloat16),
            pltpu.SemaphoreType.DMA((steps // 4,)),
            pltpu.SemaphoreType.DMA,
            pltpu.SemaphoreType.DMA((steps,)),
        ],
        input_output_aliases={} if earlier is None else {5: 0},
        compiler_params=pltpu.CompilerParams(vmem_limit_bytes=24 << 20),
        cost_estimate=pl.CostEstimate(
            flops=4 * steps * GROUP * seq * cache.shape[1] * HD,
            bytes_accessed=2 * (rows.size + cache.size + slots * seq * GROUP * HD),
            transcendentals=steps * GROUP * seq * cache.shape[1],
        ),
        name="attend",
    )(meta, cache_len, rows, cache, score, *extra)


def staged(
    step_embeds, step_len, leaf_of_step, cache_len, caches, norm_gain, qkv_weight, score_weight
):
    embeds = step_embeds[0]
    steps_here, seq, feats = embeds.shape
    leaves_here = cache_len.shape[0]
    per_leaf = steps_here // leaves_here
    peers = lax.axis_size("dp")
    me = lax.axis_index("dp")
    tensor = lax.axis_index("tensor")
    rows = peers * seq

    weights = ring_weights(qkv_weight[0])
    leaves = leaf_of_step.reshape(peers, steps_here)
    lengths = step_len.reshape(peers, steps_here)
    index = jnp.arange(steps_here, dtype=jnp.int32)
    earlier = index[None, :] < index[:, None]
    mine = lax.dynamic_index_in_dim(leaves, me, 0, keepdims=False) // leaves_here
    same = mine[None, :] == mine[:, None]
    turn = jnp.sum(same & earlier, axis=1)
    to_peer = mine[None, :] == jnp.arange(peers, dtype=jnp.int32)[:, None]
    send = [
        jnp.sum(jnp.where(to_peer & (turn == s)[None, :], index[None, :], 0), axis=1)
        for s in range(2)
    ]
    early_rows = embeds[send[0]].reshape(rows, feats)
    late_rows = embeds[send[1]]
    late_rows = lax.all_to_all(late_rows, "dp", 0, 0, tiled=True).reshape(rows, feats)

    here = (leaves // leaves_here) == me
    ordinal = jnp.sum(here[:, None, :] & earlier[None], axis=2)
    marks = jnp.stack([here & (ordinal == s) for s in range(2)])
    ids = index[None, :] + steps_here * jnp.arange(peers, dtype=jnp.int32)[:, None]
    arrive_id = jnp.sum(jnp.where(marks, ids[None], 0), axis=2).reshape(-1)
    arrive_leaf = jnp.sum(jnp.where(marks, leaves[None], 0), axis=2).reshape(-1)
    arrive_leaf = arrive_leaf - me * leaves_here
    arrive_len = jnp.sum(jnp.where(marks, lengths[None], 0), axis=2).reshape(-1)
    rank = jnp.sum(
        (arrive_leaf[None, :] == arrive_leaf[:, None])
        & (arrive_id[None, :] < arrive_id[:, None]),
        axis=1,
    )
    slot = jnp.clip(arrive_leaf * per_leaf + rank, 0, steps_here - 1)
    arrive_leaf = jnp.clip(arrive_leaf, 0, leaves_here - 1)
    meta = jnp.stack([arrive_leaf, slot, arrive_len]).astype(jnp.int32)

    a, b = early_rows, late_rows
    a_x = x_swap(a)
    a_left, a_right = y_shift(a, 1), y_shift(a, -1)
    b_left, b_right = y_shift(b, 1), y_shift(b, -1)
    b_x = x_swap(b)
    ax_left = y_shift(a_x, 1)
    ax_right = y_shift(a_x, -1)
    a_far = y_shift(a_left, 1)
    ax_far = y_shift(ax_right, -1)
    bx_left = x_swap(b_left)
    bx_right = x_swap(b_right)
    b_far = y_shift(b_right, -1)
    bx_far = y_shift(bx_left, 1)

    squares = [
        jnp.sum(jnp.square(part.astype(jnp.float32)), axis=1) for part in (a, b)
    ]

    y, h, z, core = tensor // 2, tensor % 2, me // 2, me % 2
    block = (z + jnp.array(RING, jnp.int32)) % 8
    owner = (y + jnp.array([dy for dy, _ in PLACES], jnp.int32)) % 4 * 2 + (
        h + jnp.array([dx for _, dx in PLACES], jnp.int32)
    ) % 2
    meets = owner[None, :] == block[:, None]
    start = jnp.stack([core, 1 - core]) * qkv_weight.shape[1]
    ring = jnp.arange(8, dtype=jnp.int32)

    def table_row(inside, allowed):
        local = [inside.index(p) if p in inside else -1 for p in range(8)]
        use = meets & allowed & jnp.array([v >= 0 for v in local])[None, :]
        which = jnp.sum(jnp.where(use, jnp.array(local, jnp.int32)[None, :] + 1, 0), axis=1) - 1
        used = jnp.sum(which[:, None] == ring[None, :], axis=0)
        place = jnp.cumsum(which >= 0) - 1
        order = jnp.sum(
            jnp.where((place[:, None] == ring[None, :]) & (which >= 0)[:, None], ring[:, None], 0),
            axis=0,
        )
        total = jnp.sum(which >= 0)[None]
        return jnp.concatenate([which, block, start, used, order, total]).astype(jnp.int32)

    sooner = (ring < 7)[:, None]
    a_soon, b_soon = (0, 1, 2, 3, 5, 6), (0, 1, 2, 3)
    whole = tuple(range(8))
    in_a = jnp.array([p in a_soon for p in whole])[None, :]
    in_b = jnp.array([p in b_soon for p in whole])[None, :]
    table = jnp.stack(
        [
            table_row(a_soon, sooner),
            table_row(whole, ~(sooner & in_a)),
            table_row(b_soon, sooner),
            table_row(whole, ~(sooner & in_b)),
        ]
    )
    gain = norm_gain[0].reshape(-1, feats)
    squares, table, meta, gain = lax.optimization_barrier(
        (jnp.concatenate(squares), table, (meta[:, :peers], meta[:, peers:]), gain)
    )
    sums = sent_to_all(squares, "tensor")
    sums_a, sums_b = sums[:, :rows], sums[:, rows:]
    all_a = [a, a_left, a_right, a_x, ax_left, ax_right, a_far, ax_far]
    all_b = [b, b_left, b_right, b_x, bx_left, bx_right, b_far, bx_far]
    part_a = project(
        table, 0, sums_a, gain, weights, [all_a[p] for p in a_soon], hops=7, last=False
    )
    part_b = project(
        table, 2, sums_b, gain, weights, [all_b[p] for p in b_soon], hops=7, last=False
    )
    out_a = project(table, 1, sums_a, gain, weights, all_a, acc=part_a)
    out_b = project(table, 3, sums_b, gain, weights, all_b, acc=part_b)

    out_a = lax.all_to_all(out_a.reshape(peers, seq, -1), "dp", 0, 0, tiled=True)
    out_b = out_b.reshape(peers, seq, -1)
    cache = caches[0]
    score = score_weight[0].reshape(GROUP, HD)
    context, value_b = attend(meta[1], cache_len, out_b, cache, score, steps_here)
    context, value_a = attend(
        meta[0], cache_len, out_a, cache, score, steps_here, earlier=context
    )
    contexts = context.reshape(1, leaves_here, per_leaf, seq, GROUP * HD)
    model_weight = jnp.where(lax.axis_index("mp") == 0, prior_weight, 1.0).astype(jnp.float32)
    partial = (value_a + value_b)[:, 0].reshape(leaves_here, per_leaf) * model_weight
    step_value = jnp.sum(sent_to_all(partial, ("tensor", "mp")), axis=0)
    return (contexts, step_value)


def solution(mesh):
    placed = (
        P("mp", "dp", None, "tensor"),
        P(),
        P(),
        P("dp"),
        P("mp", "dp", None, "tensor"),
        P("mp", None),
        P("mp", "dp", "tensor"),
        P("mp", "tensor"),
    )
    return jax.shard_map(
        staged,
        mesh=mesh,
        in_specs=placed,
        out_specs=(P("mp", "dp", None, None, "tensor"), P("dp", None)),
        check_vma=False,
    )
```

```python
import functools

import jax
import jax.numpy as jnp
from jax import lax
from jax.experimental import pallas as pl
from jax.experimental.pallas import tpu as pltpu
from jax.sharding import PartitionSpec as P


KVH = 8
HD = 128
HQ = 32
GROUP = HQ // KVH

prior_weight = 0.5
norm_eps = 1e-05
LOG2E = 1.4426950408889634


RING = (0, 7, 1, 6, 2, 5, 3, 4)
PLACES = ((0, 0), (-1, 0), (1, 0), (0, 1), (-1, 1), (1, 1), (2, 0), (2, 1))


def sent_to_all(value, axis):
    length = lax.axis_size(axis)
    return lax.all_to_all(
        jnp.broadcast_to(value[None], (length, *value.shape)), axis, 0, 0, tiled=True
    )


def y_shift(value, hop):
    pairs = [(y * 2 + h, ((y + hop) % 4) * 2 + h) for y in range(4) for h in range(2)]
    return lax.ppermute(value, "tensor", pairs)


def x_swap(value):
    return lax.ppermute(value, "tensor", [(t, t ^ 1) for t in range(8)])


def z_shift(value, hop):
    pairs = [(z * 2 + c, ((z + hop) % 8) * 2 + c) for z in range(8) for c in range(2)]
    return lax.ppermute(value, "dp", pairs)


def core_swap(value):
    return lax.ppermute(value, "dp", [(d, d ^ 1) for d in range(16)])


def ring_weights(shard):
    up, down = shard, shard
    found = [((0, 0), 0, shard)]
    for step in range(1, 4):
        up, down = z_shift(up, 1), z_shift(down, -1)
        found += [((2 * step - 1, step), 0, up), ((2 * step, step), 0, down)]
    found.append(((7, 4), 0, z_shift(up, 1)))
    shards = []
    for (place, step), first, value in found:
        shards.append(((place, 0, first), value))
        shards.append(((place, 1, first), core_swap(value)))
    return shards


def mm_kernel(table_ref, sums_ref, gain_ref, *rest, row, count, shards, has_acc, last, width):
    weights, rest = rest[: len(shards)], rest[len(shards) :]
    pieces, rest = rest[:count], rest[count:]
    if has_acc:
        acc_in, rest = rest[0], rest[1:]
    out_ref, xbuf, wbuf, acc, inverse, high, low, xsem, wsem, asem = rest
    part = xbuf.shape[1] // 2
    for p in range(count):

        @pl.when(table_ref[row, 18 + p] > 0)
        def _(p=p):
            pltpu.make_async_copy(pieces[p], xbuf.at[p], xsem.at[p]).start()

    for k in range(8):
        mine = [(ref, key) for ref, key in zip(weights, shards) if key[0] == k]
        if mine:

            @pl.when(table_ref[row, k] >= 0)
            def _(k=k, mine=mine):
                for ref, (_, other, first) in mine:
                    start = pl.multiple_of(table_ref[row, 16 + other] + first, 256)
                    pltpu.make_async_copy(
                        ref, wbuf.at[k, pl.ds(start, ref.shape[0])], wsem.at[k]
                    ).start()

    if has_acc:
        load = pltpu.make_async_copy(acc_in, acc, asem)
        load.start()
    total = jnp.sum(jnp.transpose(sums_ref[...]), axis=1, keepdims=True)
    inverse[...] = lax.rsqrt(total * (1.0 / width) + norm_eps)
    if has_acc:
        load.wait()
    else:
        acc[...] = jnp.zeros_like(acc)
    used = table_ref[row, 34]
    upper, lower = pl.ds(0, part), pl.ds(part, part)

    def ready(i):
        p = table_ref[row, table_ref[row, 26 + i]]
        pltpu.make_async_copy(xbuf.at[p], xbuf.at[p], xsem.at[p]).wait()

    def normed(i, at):
        k = table_ref[row, 26 + i]
        gain = gain_ref[pl.ds(table_ref[row, 8 + k], 1), :]
        x = xbuf[table_ref[row, k], at, :].astype(jnp.float32)
        return (x * inverse[at, :] * gain).astype(jnp.bfloat16)

    def visit(i, carry):
        k = table_ref[row, 26 + i]
        following = jnp.minimum(i + 1, used - 1)
        pl.when(i + 1 < used)(lambda: ready(following))
        pltpu.make_async_copy(wbuf.at[k], wbuf.at[k], wsem.at[k]).wait()
        low[...] = normed(i, lower)
        acc[upper, :] += jnp.dot(high[...], wbuf[k], preferred_element_type=jnp.float32)
        high[...] = normed(following, upper)
        acc[lower, :] += jnp.dot(low[...], wbuf[k], preferred_element_type=jnp.float32)
        return carry

    @pl.when(used > 0)
    def _():
        ready(0)
        high[...] = normed(0, upper)
        lax.fori_loop(0, used, visit, 0)

    if last:
        out_ref[...] = acc[...].astype(out_ref.dtype)
    else:
        out_ref[...] = acc[...]


def project(table, row, sums, gain, weights, pieces, hops=8, acc=None, last=True):
    weights = [pair for pair in weights if pair[0][0] < hops]
    shards = tuple(key for key, _ in weights)
    weights = [value for _, value in weights]
    blocks, feats = gain.shape
    columns = weights[0].shape[1]
    rows = sums.shape[1]
    count = len(pieces)
    smem = pl.BlockSpec(memory_space=pltpu.SMEM)
    vmem = pl.BlockSpec(memory_space=pltpu.VMEM)
    anyspace = pl.BlockSpec(memory_space=pl.ANY)
    extra = [] if acc is None else [acc]
    typical = min(count, 4)
    return pl.pallas_call(
        functools.partial(
            mm_kernel,
            row=row,
            count=count,
            shards=shards,
            has_acc=acc is not None,
            last=last,
            width=feats * blocks,
        ),
        out_shape=jax.ShapeDtypeStruct((rows, columns), jnp.bfloat16 if last else jnp.float32),
        in_specs=[smem, vmem, vmem] + [anyspace] * (len(weights) + count + len(extra)),
        out_specs=vmem,
        scratch_shapes=[
            pltpu.VMEM((count, rows, feats), jnp.bfloat16),
            pltpu.VMEM((blocks, feats, columns), jnp.bfloat16),
            pltpu.VMEM((rows, columns), jnp.float32),
            pltpu.VMEM((rows, 1), jnp.float32),
            pltpu.VMEM((rows // 2, feats), jnp.bfloat16),
            pltpu.VMEM((rows // 2, feats), jnp.bfloat16),
            pltpu.SemaphoreType.DMA((count,)),
            pltpu.SemaphoreType.DMA((blocks,)),
            pltpu.SemaphoreType.DMA,
        ],
        compiler_params=pltpu.CompilerParams(vmem_limit_bytes=44 << 20),
        cost_estimate=pl.CostEstimate(
            flops=2 * rows * columns * feats * typical,
            bytes_accessed=2 * typical * feats * (rows + columns),
            transcendentals=0,
        ),
        name="project",
    )(table, sums, gain, *weights, *pieces, *extra)


def attend_kernel(meta_ref, clen_ref, rows_hbm, cache_hbm, score_ref, *rest, seq, has_in):
    if has_in:
        rest = rest[1:]
    ctx_ref, value_ref, rows_ref, cache_ref, obuf, rsems, csem, sems = rest
    steps = rows_ref.shape[0]
    fill = pltpu.make_async_copy(cache_hbm, cache_ref, csem)
    fill.start()
    positions = cache_ref.shape[1]
    wide = GROUP * seq
    factor = (HD ** (-0.5)) * LOG2E
    token = lax.broadcasted_iota(jnp.int32, (wide, 1), 0) % seq
    column = lax.broadcasted_iota(jnp.int32, (1, positions), 1)
    causal = lax.broadcasted_iota(jnp.int32, (wide, seq), 1) <= (
        lax.broadcasted_iota(jnp.int32, (wide, seq), 0) % seq
    )
    value_ref[...] = jnp.zeros_like(value_ref)
    weights = jnp.concatenate(
        [jnp.broadcast_to(score_ref[g : g + 1, :], (seq, HD)) for g in range(GROUP)], axis=0
    )
    contract = (((1,), (1,)), ((), ()))

    together = 4

    def load(group):
        part = pl.ds(group * together, together)
        return pltpu.make_async_copy(rows_hbm.at[part], rows_ref.at[part], rsems.at[group])

    for group in range(steps // together):
        load(group).start()

    def visit(group, carry):
        load(group).wait()
        at = [group * together + k for k in range(together)]
        leaf = [meta_ref[0, i] for i in at]
        slot = [meta_ref[1, i] for i in at]
        length = [meta_ref[2, i] for i in at]
        far, own = [], []
        for i, one in zip(at, leaf):
            queries = jnp.concatenate(
                [rows_ref[i, :, g * HD : (g + 1) * HD] for g in range(GROUP)], axis=0
            )
            key_own = rows_ref[i, :, GROUP * HD : (GROUP + 1) * HD]
            far.append(
                lax.dot_general(
                    queries, cache_ref[one, :, :HD], contract, preferred_element_type=jnp.float32
                )
            )
            own.append(
                lax.dot_general(queries, key_own, contract, preferred_element_type=jnp.float32)
            )
        far = [
            f + jnp.where(column < clen_ref[one], 0.0, -jnp.inf) for f, one in zip(far, leaf)
        ]
        own = [jnp.where(causal, o, -jnp.inf) for o in own]
        top = [
            jnp.maximum(jnp.max(f, axis=1, keepdims=True), jnp.max(o, axis=1, keepdims=True))
            for f, o in zip(far, own)
        ]
        far = [jnp.exp2((f - t) * factor) for f, t in zip(far, top)]
        own = [jnp.exp2((o - t) * factor) for o, t in zip(own, top)]
        total = [
            jnp.sum(f, axis=1, keepdims=True) + jnp.sum(o, axis=1, keepdims=True)
            for f, o in zip(far, own)
        ]
        context = [
            jnp.dot(
                f.astype(jnp.bfloat16), cache_ref[one, :, HD:], preferred_element_type=jnp.float32
            )
            + jnp.dot(
                o.astype(jnp.bfloat16),
                rows_ref[i, :, (GROUP + 1) * HD :],
                preferred_element_type=jnp.float32,
            )
            for f, o, one, i in zip(far, own, leaf, at)
        ]
        for c, t, i, place, count in zip(context, total, at, slot, length):
            c = jnp.where(token < count, c * (1.0 / t), 0.0)
            for g in range(GROUP):
                obuf[i, :, g * HD : (g + 1) * HD] = c[g * seq : (g + 1) * seq].astype(
                    jnp.bfloat16
                )
            pltpu.make_async_copy(obuf.at[i], ctx_ref.at[place], sems.at[i]).start()
            scored = jnp.where(token == count - 1, c * weights, 0.0)
            scored = jnp.sum(jnp.sum(scored, axis=0, keepdims=True), axis=1, keepdims=True)
            value_ref[pl.ds(place, 1), :] = jnp.broadcast_to(scored, (1, value_ref.shape[1]))
        return carry

    fill.wait()
    lax.fori_loop(0, steps // together, visit, 0)
    for i in range(steps):
        pltpu.make_async_copy(obuf.at[i], ctx_ref.at[meta_ref[1, i]], sems.at[i]).wait()


def attend(meta, cache_len, rows, cache, score, slots, earlier=None):
    steps, seq, _ = rows.shape
    smem = pl.BlockSpec(memory_space=pltpu.SMEM)
    vmem = pl.BlockSpec(memory_space=pltpu.VMEM)
    anyspace = pl.BlockSpec(memory_space=pl.ANY)
    hbm = pl.BlockSpec(memory_space=pltpu.HBM)
    extra = [] if earlier is None else [earlier]
    return pl.pallas_call(
        functools.partial(attend_kernel, seq=seq, has_in=earlier is not None),
        out_shape=(
            jax.ShapeDtypeStruct((slots, seq, GROUP * HD), jnp.bfloat16),
            jax.ShapeDtypeStruct((slots, HD), jnp.float32),
        ),
        in_specs=[smem, smem, anyspace, hbm, vmem] + [anyspace] * len(extra),
        out_specs=(anyspace, vmem),
        scratch_shapes=[
            pltpu.VMEM(rows.shape, jnp.bfloat16),
            pltpu.VMEM(cache.shape, jnp.bfloat16),
            pltpu.VMEM((steps, seq, GROUP * HD), jnp.bfloat16),
            pltpu.SemaphoreType.DMA((steps // 4,)),
            pltpu.SemaphoreType.DMA,
            pltpu.SemaphoreType.DMA((steps,)),
        ],
        input_output_aliases={} if earlier is None else {5: 0},
        compiler_params=pltpu.CompilerParams(vmem_limit_bytes=24 << 20),
        cost_estimate=pl.CostEstimate(
            flops=4 * steps * GROUP * seq * cache.shape[1] * HD,
            bytes_accessed=2 * (rows.size + cache.size + slots * seq * GROUP * HD),
            transcendentals=steps * GROUP * seq * cache.shape[1],
        ),
        name="attend",
    )(meta, cache_len, rows, cache, score, *extra)


def staged(
    step_embeds, step_len, leaf_of_step, cache_len, caches, norm_gain, qkv_weight, score_weight
):
    embeds = step_embeds[0]
    steps_here, seq, feats = embeds.shape
    leaves_here = cache_len.shape[0]
    per_leaf = steps_here // leaves_here
    peers = lax.axis_size("dp")
    me = lax.axis_index("dp")
    tensor = lax.axis_index("tensor")
    rows = peers * seq

    weights = ring_weights(qkv_weight[0])
    leaves = leaf_of_step.reshape(peers, steps_here)
    lengths = step_len.reshape(peers, steps_here)
    index = jnp.arange(steps_here, dtype=jnp.int32)
    earlier = index[None, :] < index[:, None]
    mine = lax.dynamic_index_in_dim(leaves, me, 0, keepdims=False) // leaves_here
    same = mine[None, :] == mine[:, None]
    turn = jnp.sum(same & earlier, axis=1)
    to_peer = mine[None, :] == jnp.arange(peers, dtype=jnp.int32)[:, None]
    send = [
        jnp.sum(jnp.where(to_peer & (turn == s)[None, :], index[None, :], 0), axis=1)
        for s in range(2)
    ]
    early_rows = embeds[send[0]].reshape(rows, feats)
    late_rows = embeds[send[1]]
    late_rows = lax.all_to_all(late_rows, "dp", 0, 0, tiled=True).reshape(rows, feats)

    here = (leaves // leaves_here) == me
    ordinal = jnp.sum(here[:, None, :] & earlier[None], axis=2)
    marks = jnp.stack([here & (ordinal == s) for s in range(2)])
    ids = index[None, :] + steps_here * jnp.arange(peers, dtype=jnp.int32)[:, None]
    arrive_id = jnp.sum(jnp.where(marks, ids[None], 0), axis=2).reshape(-1)
    arrive_leaf = jnp.sum(jnp.where(marks, leaves[None], 0), axis=2).reshape(-1)
    arrive_leaf = arrive_leaf - me * leaves_here
    arrive_len = jnp.sum(jnp.where(marks, lengths[None], 0), axis=2).reshape(-1)
    rank = jnp.sum(
        (arrive_leaf[None, :] == arrive_leaf[:, None])
        & (arrive_id[None, :] < arrive_id[:, None]),
        axis=1,
    )
    slot = jnp.clip(arrive_leaf * per_leaf + rank, 0, steps_here - 1)
    arrive_leaf = jnp.clip(arrive_leaf, 0, leaves_here - 1)
    meta = jnp.stack([arrive_leaf, slot, arrive_len]).astype(jnp.int32)

    a, b = early_rows, late_rows
    a_x = x_swap(a)
    a_left, a_right = y_shift(a, 1), y_shift(a, -1)
    b_left, b_right = y_shift(b, 1), y_shift(b, -1)
    b_x = x_swap(b)
    ax_left = y_shift(a_x, 1)
    ax_right = y_shift(a_x, -1)
    a_far = y_shift(a_left, 1)
    ax_far = y_shift(ax_right, -1)
    bx_left = x_swap(b_left)
    bx_right = x_swap(b_right)
    b_far = y_shift(b_right, -1)
    bx_far = y_shift(bx_left, 1)

    squares = [
        jnp.sum(jnp.square(part.astype(jnp.float32)), axis=1) for part in (a, b)
    ]

    y, h, z, core = tensor // 2, tensor % 2, me // 2, me % 2
    block = (z + jnp.array(RING, jnp.int32)) % 8
    owner = (y + jnp.array([dy for dy, _ in PLACES], jnp.int32)) % 4 * 2 + (
        h + jnp.array([dx for _, dx in PLACES], jnp.int32)
    ) % 2
    meets = owner[None, :] == block[:, None]
    start = jnp.stack([core, 1 - core]) * qkv_weight.shape[1]
    ring = jnp.arange(8, dtype=jnp.int32)

    def table_row(inside, allowed):
        local = [inside.index(p) if p in inside else -1 for p in range(8)]
        use = meets & allowed & jnp.array([v >= 0 for v in local])[None, :]
        which = jnp.sum(jnp.where(use, jnp.array(local, jnp.int32)[None, :] + 1, 0), axis=1) - 1
        used = jnp.sum(which[:, None] == ring[None, :], axis=0)
        place = jnp.cumsum(which >= 0) - 1
        order = jnp.sum(
            jnp.where((place[:, None] == ring[None, :]) & (which >= 0)[:, None], ring[:, None], 0),
            axis=0,
        )
        total = jnp.sum(which >= 0)[None]
        return jnp.concatenate([which, block, start, used, order, total]).astype(jnp.int32)

    sooner = (ring < 7)[:, None]
    a_soon, b_soon = (0, 1, 2, 3, 5, 6), (0, 1, 2, 3)
    b_next, b_rest = (0, 1, 2, 3, 4, 5), (6, 7)
    whole = tuple(range(8))
    in_a = jnp.array([p in a_soon for p in whole])[None, :]
    in_b = jnp.array([p in b_soon for p in whole])[None, :]
    table = jnp.stack(
        [
            table_row(a_soon, sooner),
            table_row(whole, ~(sooner & in_a)),
            table_row(b_soon, sooner),
            table_row(b_next, ~(sooner & in_b)),
            table_row(b_rest, ring[:, None] >= 0),
        ]
    )
    gain = norm_gain[0].reshape(-1, feats)
    squares, table, meta, gain = lax.optimization_barrier(
        (jnp.concatenate(squares), table, (meta[:, :peers], meta[:, peers:]), gain)
    )
    sums = sent_to_all(squares, "tensor")
    sums_a, sums_b = sums[:, :rows], sums[:, rows:]
    all_a = [a, a_left, a_right, a_x, ax_left, ax_right, a_far, ax_far]
    all_b = [b, b_left, b_right, b_x, bx_left, bx_right, b_far, bx_far]
    part_a = project(
        table, 0, sums_a, gain, weights, [all_a[p] for p in a_soon], hops=7, last=False
    )
    part_b = project(
        table, 2, sums_b, gain, weights, [all_b[p] for p in b_soon], hops=7, last=False
    )
    out_a = project(table, 1, sums_a, gain, weights, all_a, acc=part_a)
    part_b = project(
        table, 3, sums_b, gain, weights, [all_b[p] for p in b_next], acc=part_b, last=False
    )
    out_b = project(table, 4, sums_b, gain, weights, [all_b[p] for p in b_rest], acc=part_b)

    out_a = lax.all_to_all(out_a.reshape(peers, seq, -1), "dp", 0, 0, tiled=True)
    out_b = out_b.reshape(peers, seq, -1)
    cache = caches[0]
    score = score_weight[0].reshape(GROUP, HD)
    context, value_b = attend(meta[1], cache_len, out_b, cache, score, steps_here)
    context, value_a = attend(
        meta[0], cache_len, out_a, cache, score, steps_here, earlier=context
    )
    contexts = context.reshape(1, leaves_here, per_leaf, seq, GROUP * HD)
    model_weight = jnp.where(lax.axis_index("mp") == 0, prior_weight, 1.0).astype(jnp.float32)
    partial = (value_a + value_b)[:, 0].reshape(leaves_here, per_leaf) * model_weight
    step_value = jnp.sum(sent_to_all(partial, ("tensor", "mp")), axis=0)
    return (contexts, step_value)


def solution(mesh):
    placed = (
        P("mp", "dp", None, "tensor"),
        P(),
        P(),
        P("dp"),
        P("mp", "dp", None, "tensor"),
        P("mp", None),
        P("mp", "dp", "tensor"),
        P("mp", "tensor"),
    )
    return jax.shard_map(
        staged,
        mesh=mesh,
        in_specs=placed,
        out_specs=(P("mp", "dp", None, None, "tensor"), P("dp", None)),
        check_vma=False,
    )
```

```python
import functools

import jax
import jax.numpy as jnp
from jax import lax
from jax.experimental import pallas as pl
from jax.experimental.pallas import tpu as pltpu
from jax.sharding import PartitionSpec as P


KVH = 8
HD = 128
HQ = 32
GROUP = HQ // KVH

prior_weight = 0.5
norm_eps = 1e-05
LOG2E = 1.4426950408889634


RING = (0, 7, 1, 6, 2, 5, 3, 4)
PLACES = ((0, 0), (-1, 0), (1, 0), (0, 1), (-1, 1), (1, 1), (2, 0), (2, 1))


def sent_to_all(value, axis):
    length = lax.axis_size(axis)
    return lax.all_to_all(
        jnp.broadcast_to(value[None], (length, *value.shape)), axis, 0, 0, tiled=True
    )


def y_shift(value, hop):
    pairs = [(y * 2 + h, ((y + hop) % 4) * 2 + h) for y in range(4) for h in range(2)]
    return lax.ppermute(value, "tensor", pairs)


def x_swap(value):
    return lax.ppermute(value, "tensor", [(t, t ^ 1) for t in range(8)])


def z_shift(value, hop):
    pairs = [(z * 2 + c, ((z + hop) % 8) * 2 + c) for z in range(8) for c in range(2)]
    return lax.ppermute(value, "dp", pairs)


def core_swap(value):
    return lax.ppermute(value, "dp", [(d, d ^ 1) for d in range(16)])


def ring_weights(shard):
    up, down = shard, shard
    found = [((0, 0), 0, shard)]
    for step in range(1, 4):
        up, down = z_shift(up, 1), z_shift(down, -1)
        found += [((2 * step - 1, step), 0, up), ((2 * step, step), 0, down)]
    found.append(((7, 4), 0, z_shift(up, 1)))
    shards = []
    for (place, step), first, value in found:
        shards.append(((place, 0, first), value))
        shards.append(((place, 1, first), core_swap(value)))
    return shards


def add_pieces(
    table_ref, row, gain_ref, first, before, xbuf, wbuf, acc, inverse, high, low, xsem, wsem
):
    part = acc.shape[0] // 2
    used = table_ref[row, 34]
    upper, lower = pl.ds(0, part), pl.ds(part, part)

    def ready(i):
        p = table_ref[row, table_ref[row, 26 + i]] + first
        pltpu.make_async_copy(xbuf.at[p], xbuf.at[p], xsem.at[p]).wait()

    def normed(i, at):
        k = table_ref[row, 26 + i]
        gain = gain_ref[pl.ds(table_ref[row, 8 + k], 1), :]
        x = xbuf[table_ref[row, k] + first, at, :].astype(jnp.float32)
        return (x * inverse[at, :] * gain).astype(jnp.bfloat16)

    def visit(i, carry):
        k = table_ref[row, 26 + i]
        following = jnp.minimum(i + 1, used - 1)
        pl.when(i + 1 < used)(lambda: ready(following))
        arrive = pltpu.make_async_copy(wbuf.at[k], wbuf.at[k], wsem.at[k])
        if before is None:
            arrive.wait()
        else:
            pl.when(table_ref[before, k] < 0)(arrive.wait)
        low[...] = normed(i, lower)
        acc[upper, :] += jnp.dot(high[...], wbuf[k], preferred_element_type=jnp.float32)
        high[...] = normed(following, upper)
        acc[lower, :] += jnp.dot(low[...], wbuf[k], preferred_element_type=jnp.float32)
        return carry

    @pl.when(used > 0)
    def _():
        ready(0)
        high[...] = normed(0, upper)
        lax.fori_loop(0, used, visit, 0)


def soon_kernel(table_ref, sums_a, sums_b, gain_ref, *rest, rows, counts, shards, width):
    weights, rest = rest[: len(shards)], rest[len(shards) :]
    pieces, rest = rest[: sum(counts)], rest[sum(counts) :]
    out_a, out_b, xbuf, wbuf, inverse, high, low, xsem, wsem = rest
    row_a, row_b = rows
    for p in range(sum(counts)):
        row, at = (row_a, p) if p < counts[0] else (row_b, p - counts[0])

        @pl.when(table_ref[row, 18 + at] > 0)
        def _(p=p):
            pltpu.make_async_copy(pieces[p], xbuf.at[p], xsem.at[p]).start()

    for k in range(8):
        mine = [(ref, key) for ref, key in zip(weights, shards) if key[0] == k]
        if mine:

            @pl.when((table_ref[row_a, k] >= 0) | (table_ref[row_b, k] >= 0))
            def _(k=k, mine=mine):
                for ref, (_, other, first) in mine:
                    start = pl.multiple_of(table_ref[row_a, 16 + other] + first, 256)
                    pltpu.make_async_copy(
                        ref, wbuf.at[k, pl.ds(start, ref.shape[0])], wsem.at[k]
                    ).start()

    parts = ((row_a, 0, None, sums_a, out_a), (row_b, counts[0], row_a, sums_b, out_b))
    for row, first, before, sums_ref, out in parts:
        total = jnp.sum(jnp.transpose(sums_ref[...]), axis=1, keepdims=True)
        inverse[...] = lax.rsqrt(total * (1.0 / width) + norm_eps)
        out[...] = jnp.zeros_like(out)
        add_pieces(
            table_ref, row, gain_ref, first, before, xbuf, wbuf, out, inverse, high, low, xsem, wsem
        )


def project_soon(table, rows, sums, gain, weights, pieces, hops):
    weights = [pair for pair in weights if pair[0][0] < hops]
    shards = tuple(key for key, _ in weights)
    weights = [value for _, value in weights]
    blocks, feats = gain.shape
    columns = weights[0].shape[1]
    height = sums[0].shape[1]
    counts = tuple(len(part) for part in pieces)
    smem = pl.BlockSpec(memory_space=pltpu.SMEM)
    vmem = pl.BlockSpec(memory_space=pltpu.VMEM)
    anyspace = pl.BlockSpec(memory_space=pl.ANY)
    shape = jax.ShapeDtypeStruct((height, columns), jnp.float32)
    return pl.pallas_call(
        functools.partial(
            soon_kernel, rows=rows, counts=counts, shards=shards, width=feats * blocks
        ),
        out_shape=(shape, shape),
        in_specs=[smem, vmem, vmem, vmem] + [anyspace] * (len(weights) + sum(counts)),
        out_specs=(vmem, vmem),
        scratch_shapes=[
            pltpu.VMEM((sum(counts), height, feats), jnp.bfloat16),
            pltpu.VMEM((blocks, feats, columns), jnp.bfloat16),
            pltpu.VMEM((height, 1), jnp.float32),
            pltpu.VMEM((height // 2, feats), jnp.bfloat16),
            pltpu.VMEM((height // 2, feats), jnp.bfloat16),
            pltpu.SemaphoreType.DMA((sum(counts),)),
            pltpu.SemaphoreType.DMA((blocks,)),
        ],
        compiler_params=pltpu.CompilerParams(vmem_limit_bytes=44 << 20),
        cost_estimate=pl.CostEstimate(
            flops=2 * height * columns * feats * 8,
            bytes_accessed=16 * feats * (height + columns),
            transcendentals=0,
        ),
        name="project_soon",
    )(table, *sums, gain, *weights, *pieces[0], *pieces[1])


def mm_kernel(table_ref, sums_ref, gain_ref, *rest, row, count, shards, has_acc, last, width):
    weights, rest = rest[: len(shards)], rest[len(shards) :]
    pieces, rest = rest[:count], rest[count:]
    if has_acc:
        acc_in, rest = rest[0], rest[1:]
    out_ref, xbuf, wbuf, acc, inverse, high, low, xsem, wsem, asem = rest
    for p in range(count):

        @pl.when(table_ref[row, 18 + p] > 0)
        def _(p=p):
            pltpu.make_async_copy(pieces[p], xbuf.at[p], xsem.at[p]).start()

    for k in range(8):
        mine = [(ref, key) for ref, key in zip(weights, shards) if key[0] == k]
        if mine:

            @pl.when(table_ref[row, k] >= 0)
            def _(k=k, mine=mine):
                for ref, (_, other, first) in mine:
                    start = pl.multiple_of(table_ref[row, 16 + other] + first, 256)
                    pltpu.make_async_copy(
                        ref, wbuf.at[k, pl.ds(start, ref.shape[0])], wsem.at[k]
                    ).start()

    if has_acc:
        load = pltpu.make_async_copy(acc_in, acc, asem)
        load.start()
    total = jnp.sum(jnp.transpose(sums_ref[...]), axis=1, keepdims=True)
    inverse[...] = lax.rsqrt(total * (1.0 / width) + norm_eps)
    if has_acc:
        load.wait()
    else:
        acc[...] = jnp.zeros_like(acc)
    add_pieces(table_ref, row, gain_ref, 0, None, xbuf, wbuf, acc, inverse, high, low, xsem, wsem)
    if last:
        out_ref[...] = acc[...].astype(out_ref.dtype)
    else:
        out_ref[...] = acc[...]


def project(table, row, sums, gain, weights, pieces, hops=8, acc=None, last=True):
    weights = [pair for pair in weights if pair[0][0] < hops]
    shards = tuple(key for key, _ in weights)
    weights = [value for _, value in weights]
    blocks, feats = gain.shape
    columns = weights[0].shape[1]
    rows = sums.shape[1]
    count = len(pieces)
    smem = pl.BlockSpec(memory_space=pltpu.SMEM)
    vmem = pl.BlockSpec(memory_space=pltpu.VMEM)
    anyspace = pl.BlockSpec(memory_space=pl.ANY)
    extra = [] if acc is None else [acc]
    typical = min(count, 4)
    return pl.pallas_call(
        functools.partial(
            mm_kernel,
            row=row,
            count=count,
            shards=shards,
            has_acc=acc is not None,
            last=last,
            width=feats * blocks,
        ),
        out_shape=jax.ShapeDtypeStruct((rows, columns), jnp.bfloat16 if last else jnp.float32),
        in_specs=[smem, vmem, vmem] + [anyspace] * (len(weights) + count + len(extra)),
        out_specs=vmem,
        scratch_shapes=[
            pltpu.VMEM((count, rows, feats), jnp.bfloat16),
            pltpu.VMEM((blocks, feats, columns), jnp.bfloat16),
            pltpu.VMEM((rows, columns), jnp.float32),
            pltpu.VMEM((rows, 1), jnp.float32),
            pltpu.VMEM((rows // 2, feats), jnp.bfloat16),
            pltpu.VMEM((rows // 2, feats), jnp.bfloat16),
            pltpu.SemaphoreType.DMA((count,)),
            pltpu.SemaphoreType.DMA((blocks,)),
            pltpu.SemaphoreType.DMA,
        ],
        compiler_params=pltpu.CompilerParams(vmem_limit_bytes=44 << 20),
        cost_estimate=pl.CostEstimate(
            flops=2 * rows * columns * feats * typical,
            bytes_accessed=2 * typical * feats * (rows + columns),
            transcendentals=0,
        ),
        name="project",
    )(table, sums, gain, *weights, *pieces, *extra)


def attend_kernel(meta_ref, clen_ref, rows_hbm, cache_hbm, score_ref, *rest, seq, has_in):
    if has_in:
        rest = rest[1:]
    ctx_ref, value_ref, rows_ref, cache_ref, obuf, rsems, csem, sems = rest
    steps = rows_ref.shape[0]
    fill = pltpu.make_async_copy(cache_hbm, cache_ref, csem)
    fill.start()
    positions = cache_ref.shape[1]
    wide = GROUP * seq
    factor = (HD ** (-0.5)) * LOG2E
    token = lax.broadcasted_iota(jnp.int32, (wide, 1), 0) % seq
    column = lax.broadcasted_iota(jnp.int32, (1, positions), 1)
    causal = lax.broadcasted_iota(jnp.int32, (wide, HD), 1) <= (
        lax.broadcasted_iota(jnp.int32, (wide, HD), 0) % seq
    )
    blank = jnp.zeros((HD - seq, HD), jnp.bfloat16)
    value_ref[...] = jnp.zeros_like(value_ref)
    weights = jnp.concatenate(
        [jnp.broadcast_to(score_ref[g : g + 1, :], (seq, HD)) for g in range(GROUP)], axis=0
    )
    contract = (((1,), (1,)), ((), ()))

    together = 4

    def load(group):
        part = pl.ds(group * together, together)
        return pltpu.make_async_copy(rows_hbm.at[part], rows_ref.at[part], rsems.at[group])

    for group in range(steps // together):
        load(group).start()

    def visit(group, carry):
        load(group).wait()
        at = [group * together + k for k in range(together)]
        leaf = [meta_ref[0, i] for i in at]
        slot = [meta_ref[1, i] for i in at]
        length = [meta_ref[2, i] for i in at]
        scores = []
        for i, one in zip(at, leaf):
            queries = jnp.concatenate(
                [rows_ref[i, :, g * HD : (g + 1) * HD] for g in range(GROUP)], axis=0
            )
            key_own = jnp.concatenate(
                [rows_ref[i, :, GROUP * HD : (GROUP + 1) * HD], blank], axis=0
            )
            far = lax.dot_general(
                queries, cache_ref[one, :, :HD], contract, preferred_element_type=jnp.float32
            )
            own = lax.dot_general(
                queries, key_own, contract, preferred_element_type=jnp.float32
            )
            far = far + jnp.where(column < clen_ref[one], 0.0, -jnp.inf)
            own = jnp.where(causal, own, -jnp.inf)
            scores.append(jnp.concatenate([far, own], axis=1))
        top = [jnp.max(v, axis=1, keepdims=True) for v in scores]
        probs = [jnp.exp2((v - t) * factor) for v, t in zip(scores, top)]
        total = [jnp.sum(v, axis=1, keepdims=True) for v in probs]
        context = []
        for v, one, i in zip(probs, leaf, at):
            rounded = v.astype(jnp.bfloat16)
            value_own = jnp.concatenate([rows_ref[i, :, (GROUP + 1) * HD :], blank], axis=0)
            context.append(
                jnp.dot(
                    rounded[:, :positions],
                    cache_ref[one, :, HD:],
                    preferred_element_type=jnp.float32,
                )
                + jnp.dot(rounded[:, positions:], value_own, preferred_element_type=jnp.float32)
            )
        for c, t, i, place, count in zip(context, total, at, slot, length):
            c = jnp.where(token < count, c * (1.0 / t), 0.0)
            for g in range(GROUP):
                obuf[i, :, g * HD : (g + 1) * HD] = c[g * seq : (g + 1) * seq].astype(
                    jnp.bfloat16
                )
            pltpu.make_async_copy(obuf.at[i], ctx_ref.at[place], sems.at[i]).start()
            scored = jnp.where(token == count - 1, c * weights, 0.0)
            scored = jnp.sum(jnp.sum(scored, axis=0, keepdims=True), axis=1, keepdims=True)
            value_ref[pl.ds(place, 1), :] = jnp.broadcast_to(scored, (1, value_ref.shape[1]))
        return carry

    fill.wait()
    lax.fori_loop(0, steps // together, visit, 0)
    for i in range(steps):
        pltpu.make_async_copy(obuf.at[i], ctx_ref.at[meta_ref[1, i]], sems.at[i]).wait()


def attend(meta, cache_len, rows, cache, score, slots, earlier=None):
    steps, seq, _ = rows.shape
    smem = pl.BlockSpec(memory_space=pltpu.SMEM)
    vmem = pl.BlockSpec(memory_space=pltpu.VMEM)
    anyspace = pl.BlockSpec(memory_space=pl.ANY)
    hbm = pl.BlockSpec(memory_space=pltpu.HBM)
    extra = [] if earlier is None else [earlier]
    return pl.pallas_call(
        functools.partial(attend_kernel, seq=seq, has_in=earlier is not None),
        out_shape=(
            jax.ShapeDtypeStruct((slots, seq, GROUP * HD), jnp.bfloat16),
            jax.ShapeDtypeStruct((slots, HD), jnp.float32),
        ),
        in_specs=[smem, smem, anyspace, hbm, vmem] + [anyspace] * len(extra),
        out_specs=(anyspace, vmem),
        scratch_shapes=[
            pltpu.VMEM(rows.shape, jnp.bfloat16),
            pltpu.VMEM(cache.shape, jnp.bfloat16),
            pltpu.VMEM((steps, seq, GROUP * HD), jnp.bfloat16),
            pltpu.SemaphoreType.DMA((steps // 4,)),
            pltpu.SemaphoreType.DMA,
            pltpu.SemaphoreType.DMA((steps,)),
        ],
        input_output_aliases={} if earlier is None else {5: 0},
        compiler_params=pltpu.CompilerParams(vmem_limit_bytes=24 << 20),
        cost_estimate=pl.CostEstimate(
            flops=4 * steps * GROUP * seq * cache.shape[1] * HD,
            bytes_accessed=2 * (rows.size + cache.size + slots * seq * GROUP * HD),
            transcendentals=steps * GROUP * seq * cache.shape[1],
        ),
        name="attend",
    )(meta, cache_len, rows, cache, score, *extra)


def staged(
    step_embeds, step_len, leaf_of_step, cache_len, caches, norm_gain, qkv_weight, score_weight
):
    embeds = step_embeds[0]
    steps_here, seq, feats = embeds.shape
    leaves_here = cache_len.shape[0]
    per_leaf = steps_here // leaves_here
    peers = lax.axis_size("dp")
    me = lax.axis_index("dp")
    tensor = lax.axis_index("tensor")
    rows = peers * seq

    weights = ring_weights(qkv_weight[0])
    leaves = leaf_of_step.reshape(peers, steps_here)
    lengths = step_len.reshape(peers, steps_here)
    index = jnp.arange(steps_here, dtype=jnp.int32)
    earlier = index[None, :] < index[:, None]
    mine = lax.dynamic_index_in_dim(leaves, me, 0, keepdims=False) // leaves_here
    same = mine[None, :] == mine[:, None]
    turn = jnp.sum(same & earlier, axis=1)
    to_peer = mine[None, :] == jnp.arange(peers, dtype=jnp.int32)[:, None]
    send = [
        jnp.sum(jnp.where(to_peer & (turn == s)[None, :], index[None, :], 0), axis=1)
        for s in range(2)
    ]
    early_rows = embeds[send[0]].reshape(rows, feats)
    late_rows = embeds[send[1]]
    late_rows = lax.all_to_all(late_rows, "dp", 0, 0, tiled=True).reshape(rows, feats)

    here = (leaves // leaves_here) == me
    ordinal = jnp.sum(here[:, None, :] & earlier[None], axis=2)
    marks = jnp.stack([here & (ordinal == s) for s in range(2)])
    ids = index[None, :] + steps_here * jnp.arange(peers, dtype=jnp.int32)[:, None]
    arrive_id = jnp.sum(jnp.where(marks, ids[None], 0), axis=2).reshape(-1)
    arrive_leaf = jnp.sum(jnp.where(marks, leaves[None], 0), axis=2).reshape(-1)
    arrive_leaf = arrive_leaf - me * leaves_here
    arrive_len = jnp.sum(jnp.where(marks, lengths[None], 0), axis=2).reshape(-1)
    rank = jnp.sum(
        (arrive_leaf[None, :] == arrive_leaf[:, None])
        & (arrive_id[None, :] < arrive_id[:, None]),
        axis=1,
    )
    slot = jnp.clip(arrive_leaf * per_leaf + rank, 0, steps_here - 1)
    arrive_leaf = jnp.clip(arrive_leaf, 0, leaves_here - 1)
    meta = jnp.stack([arrive_leaf, slot, arrive_len]).astype(jnp.int32)

    a, b = early_rows, late_rows
    a_x = x_swap(a)
    a_left, a_right = y_shift(a, 1), y_shift(a, -1)
    b_left, b_right = y_shift(b, 1), y_shift(b, -1)
    b_x = x_swap(b)
    ax_left = y_shift(a_x, 1)
    ax_right = y_shift(a_x, -1)
    a_far = y_shift(a_left, 1)
    ax_far = y_shift(ax_right, -1)
    bx_left = x_swap(b_left)
    bx_right = x_swap(b_right)
    b_far = y_shift(b_right, -1)
    bx_far = y_shift(bx_left, 1)

    squares = [
        jnp.sum(jnp.square(part.astype(jnp.float32)), axis=1) for part in (a, b)
    ]

    y, h, z, core = tensor // 2, tensor % 2, me // 2, me % 2
    block = (z + jnp.array(RING, jnp.int32)) % 8
    owner = (y + jnp.array([dy for dy, _ in PLACES], jnp.int32)) % 4 * 2 + (
        h + jnp.array([dx for _, dx in PLACES], jnp.int32)
    ) % 2
    meets = owner[None, :] == block[:, None]
    start = jnp.stack([core, 1 - core]) * qkv_weight.shape[1]
    ring = jnp.arange(8, dtype=jnp.int32)

    def table_row(inside, allowed):
        local = [inside.index(p) if p in inside else -1 for p in range(8)]
        use = meets & allowed & jnp.array([v >= 0 for v in local])[None, :]
        which = jnp.sum(jnp.where(use, jnp.array(local, jnp.int32)[None, :] + 1, 0), axis=1) - 1
        used = jnp.sum(which[:, None] == ring[None, :], axis=0)
        place = jnp.cumsum(which >= 0) - 1
        order = jnp.sum(
            jnp.where((place[:, None] == ring[None, :]) & (which >= 0)[:, None], ring[:, None], 0),
            axis=0,
        )
        total = jnp.sum(which >= 0)[None]
        return jnp.concatenate([which, block, start, used, order, total]).astype(jnp.int32)

    sooner = (ring < 7)[:, None]
    a_soon, b_soon = (0, 1, 2, 3, 5, 6), (0, 1, 2, 3)
    b_next, b_rest = (0, 1, 2, 3, 4, 5), (6, 7)
    whole = tuple(range(8))
    in_a = jnp.array([p in a_soon for p in whole])[None, :]
    in_b = jnp.array([p in b_soon for p in whole])[None, :]
    table = jnp.stack(
        [
            table_row(a_soon, sooner),
            table_row(whole, ~(sooner & in_a)),
            table_row(b_soon, sooner),
            table_row(b_next, ~(sooner & in_b)),
            table_row(b_rest, ring[:, None] >= 0),
        ]
    )
    gain = norm_gain[0].reshape(-1, feats)
    squares, table, meta, gain = lax.optimization_barrier(
        (jnp.concatenate(squares), table, (meta[:, :peers], meta[:, peers:]), gain)
    )
    sums = sent_to_all(squares, "tensor")
    sums_a, sums_b = sums[:, :rows], sums[:, rows:]
    all_a = [a, a_left, a_right, a_x, ax_left, ax_right, a_far, ax_far]
    all_b = [b, b_left, b_right, b_x, bx_left, bx_right, b_far, bx_far]
    part_a, part_b = project_soon(
        table,
        (0, 2),
        (sums_a, sums_b),
        gain,
        weights,
        ([all_a[p] for p in a_soon], [all_b[p] for p in b_soon]),
        hops=7,
    )
    out_a = project(table, 1, sums_a, gain, weights, all_a, acc=part_a)
    part_b = project(
        table, 3, sums_b, gain, weights, [all_b[p] for p in b_next], acc=part_b, last=False
    )
    out_b = project(table, 4, sums_b, gain, weights, [all_b[p] for p in b_rest], acc=part_b)

    out_a = lax.all_to_all(out_a.reshape(peers, seq, -1), "dp", 0, 0, tiled=True)
    out_b = out_b.reshape(peers, seq, -1)
    cache = caches[0]
    score = score_weight[0].reshape(GROUP, HD)
    context, value_b = attend(meta[1], cache_len, out_b, cache, score, steps_here)
    context, value_a = attend(
        meta[0], cache_len, out_a, cache, score, steps_here, earlier=context
    )
    contexts = context.reshape(1, leaves_here, per_leaf, seq, GROUP * HD)
    model_weight = jnp.where(lax.axis_index("mp") == 0, prior_weight, 1.0).astype(jnp.float32)
    partial = (value_a + value_b)[:, 0].reshape(leaves_here, per_leaf) * model_weight
    step_value = jnp.sum(sent_to_all(partial, ("tensor", "mp")), axis=0)
    return (contexts, step_value)


def solution(mesh):
    placed = (
        P("mp", "dp", None, "tensor"),
        P(),
        P(),
        P("dp"),
        P("mp", "dp", None, "tensor"),
        P("mp", None),
        P("mp", "dp", "tensor"),
        P("mp", "tensor"),
    )
    return jax.shard_map(
        staged,
        mesh=mesh,
        in_specs=placed,
        out_specs=(P("mp", "dp", None, None, "tensor"), P("dp", None)),
        check_vma=False,
    )
```
